256 devices in a mesh: dp: 16 (over z, core), expert: 16 (over y, x).
Axes of the slice: x: 4, y: 4, z: 8, core: 2. Of those that a mesh axis runs over, the one named last changes fastest.
Arguments:
- tokens: bfloat16 [65536, 1024], P(('dp', 'expert')), may hold values from -6 to 6
- cotangent: bfloat16 [65536, 1024], P(('dp', 'expert')), may hold values from -6 to 6
- route_logits: float32 [65536, 2], P(('dp', 'expert')), may hold values from -6 to 6
- expert_ids: int32 [65536, 2], P(('dp', 'expert')), may hold values from 0 to 31, as said below
- slot_pos: int32 [65536, 2], P(('dp', 'expert')), may hold values from 0 to 31, as said below
- w_in: bfloat16 [32, 1024, 1536], P('expert'), may hold values from -0.1875 to 0.1875
- w_down: bfloat16 [32, 768, 1024], P('expert'), may hold values from -0.21875 to 0.21875
Outputs:
- input_grad: bfloat16 [65536, 1024], P(('dp', 'expert'))
- grad_in: float32 [32, 1024, 1536], P('expert', 'dp')
- grad_down: float32 [32, 768, 1024], P('expert', 'dp')
The draws below stay inside these ranges and needn't reach their ends.
Inputs may be any that keep to these rules, and one draw needn't show every extreme that they name: `expert_ids`: each row names 2 different experts. Within each aligned block of 256 rows (the tokens of one device) no expert is named more than 32 times, and one expert, the same in all blocks, is named exactly 32 times in every block. `slot_pos`: within each aligned block of 256 rows, entries whose matching expert_ids entries name the same expert are distinct.
All inputs are finite; a program needn't handle non-finite values.
Results may differ from the reference program's by a relative error of at most 0.02.
Values may be sent and summed in bfloat16 or wider, within the bound.
A program may use at most 128 MiB of HBM per device.

```python
import jax
import jax.numpy as jnp
from jax import lax

D = 1024
FF = 768
TOP = 2
TOK_DEV = 256
EXPERTS = 32
CAP = 32
TOKENS = 65536
N_DP = 16
N_EXPERT = 16


def routing_tables(key):
    blocks = TOKENS // TOK_DEV
    favored = jax.random.randint(jax.random.fold_in(key, 7), (), 0, EXPERTS)
    labels = jnp.arange(EXPERTS, dtype=jnp.int32)
    is_full = labels == favored
    positions = jnp.arange(TOP * TOK_DEV, dtype=jnp.int32)
    remainder = TOP * TOK_DEV - CAP

    def shuffled(slot_key):
        return jax.random.permutation(slot_key, CAP).astype(jnp.int32)

    def one_block(index):
        block_key = jax.random.fold_in(jax.random.fold_in(key, 11), index)
        key_weight, key_order, key_slots, key_tokens = jax.random.split(block_key, 4)
        weights = jnp.where(is_full, 0, jax.random.randint(key_weight, (EXPERTS,), 2, 5)).astype(jnp.int32)
        shares = (weights * remainder // jnp.sum(weights)).astype(jnp.int32)
        leftover = remainder - jnp.sum(shares)
        order = jax.random.permutation(key_order, EXPERTS).astype(jnp.int32)
        ranking = jnp.zeros((EXPERTS,), jnp.int32).at[order].set(labels)
        full_rank = jnp.sum(jnp.where(is_full, ranking, 0))
        other_rank = ranking - (ranking > full_rank).astype(jnp.int32)
        extra = jnp.logical_and(jnp.logical_not(is_full), other_rank < leftover).astype(jnp.int32)
        counts = jnp.where(is_full, CAP, shares + extra).astype(jnp.int32)
        ends = jnp.cumsum(counts).astype(jnp.int32)
        starts = ends - counts
        label_at = jnp.sum((ends[None, :] <= positions[:, None]).astype(jnp.int32), axis=1)
        within = positions - starts[label_at]
        tables = jax.vmap(shuffled)(jax.random.split(key_slots, EXPERTS))
        slot_at = tables[label_at, within]
        ids_block = label_at.reshape(TOP, TOK_DEV).T
        slots_block = slot_at.reshape(TOP, TOK_DEV).T
        mixing = jax.random.permutation(key_tokens, TOK_DEV)
        return (ids_block[mixing], slots_block[mixing])
    chosen, places = lax.map(one_block, jnp.arange(blocks, dtype=jnp.int32))
    return (chosen.reshape(TOKENS, TOP).astype(jnp.int32), places.reshape(TOKENS, TOP).astype(jnp.int32))


def draw_expert_ids(key, part):
    return routing_tables(jax.random.fold_in(key, 3))[0]


def draw_slot_pos(key, part):
    return routing_tables(jax.random.fold_in(key, 3))[1]


def block_levels(key, dims, cuts, low, top_value):
    gain = 1.0
    for dim, parts in cuts:
        heights = jax.random.uniform(jax.random.fold_in(jax.random.fold_in(key, 6), dim), (parts,), jnp.float32, low / len(cuts), top_value / len(cuts))
        gain = gain * jnp.repeat(jnp.exp(heights), dims[dim] // parts).reshape((-1,) + (1,) * (len(dims) - 1 - dim))
    return gain


def normal_values(stream_key, extent, spread, limit, cuts=(), kind=jnp.bfloat16):
    values = spread * jax.random.normal(stream_key, extent, jnp.float32)
    if cuts:
        values = values * block_levels(stream_key, extent, cuts, -0.22, 0.18)
    return jnp.clip(values, -limit, limit).astype(kind)


def setup_inputs(seed: int = 0) -> dict:
    streams_of = jax.random.split(jax.random.key(seed), 8)
    tokens = normal_values(streams_of[0], (TOKENS, D), 1.0, 6.0, ((0, 256),))
    cotangent = normal_values(streams_of[1], (TOKENS, D), 1.0, 6.0, ((0, 256),))
    route_logits = normal_values(streams_of[2], (TOKENS, TOP), 1.5, 6.0, ((0, 256),), jnp.float32)
    expert_ids = draw_expert_ids(jax.random.fold_in(streams_of[7], 71), 0)
    slot_pos = draw_slot_pos(jax.random.fold_in(streams_of[7], 71), 0)
    w_in = normal_values(streams_of[5], (EXPERTS, D, 2 * FF), D ** -0.5, 0.1875, ((0, 16),))
    w_down = normal_values(streams_of[6], (EXPERTS, FF, D), FF ** -0.5, 0.21875, ((0, 16),))
    return dict(tokens=tokens, cotangent=cotangent, route_logits=route_logits, expert_ids=expert_ids, slot_pos=slot_pos, w_in=w_in, w_down=w_down)


def reference(tokens, cotangent, route_logits, expert_ids, slot_pos, w_in, w_down):
    group_rows = N_EXPERT * TOK_DEV
    slots_all = N_EXPERT * CAP
    w_in_wide = w_in.astype(jnp.float32)
    w_down_wide = w_down.astype(jnp.float32)
    source = (jnp.arange(group_rows, dtype=jnp.int32) // TOK_DEV) * CAP

    def one_group(carry, group):
        sum_in, sum_down = carry
        inputs, cotan, logits, chosen, places = group
        first = jax.nn.sigmoid(logits[:, 0] - logits[:, 1])
        combine = jnp.stack([first, 1.0 - first], axis=1)
        scaled = (combine[:, :, None] * cotan[:, None, :].astype(jnp.float32)).astype(jnp.bfloat16)
        scaled = lax.optimization_barrier(scaled)
        destination = (chosen.astype(jnp.int32) * slots_all + source[:, None] + places.astype(jnp.int32)).reshape(-1)
        empty = jnp.zeros((EXPERTS * slots_all, D), jnp.bfloat16)
        repeated = jnp.broadcast_to(inputs[:, None, :], (group_rows, TOP, D)).reshape(-1, D)
        input_slots = empty.at[destination].set(repeated).reshape(EXPERTS, slots_all, D).astype(jnp.float32)
        cotangent_slots = empty.at[destination].set(scaled.reshape(-1, D)).reshape(EXPERTS, slots_all, D).astype(jnp.float32)
        gate_up = jnp.einsum("esd,edf->esf", input_slots, w_in_wide)
        gate = gate_up[:, :, :FF]
        upper = gate_up[:, :, FF:]
        sigmoid_gate = jax.nn.sigmoid(gate)
        activated = gate * sigmoid_gate
        hidden = lax.optimization_barrier((activated * upper).astype(jnp.bfloat16)).astype(jnp.float32)
        grad_hidden = jnp.einsum("esd,efd->esf", cotangent_slots, w_down_wide)
        grad_gate = grad_hidden * upper * sigmoid_gate * (1.0 + gate * (1.0 - sigmoid_gate))
        grad_up = grad_hidden * activated
        grad_pair = jnp.concatenate([grad_gate, grad_up], axis=2).astype(jnp.bfloat16)
        grad_pair = lax.optimization_barrier(grad_pair).astype(jnp.float32)
        term_down = jnp.einsum("esf,esd->efd", hidden, cotangent_slots)
        term_in = jnp.einsum("esd,esf->edf", input_slots, grad_pair)
        returned = jnp.einsum("esf,edf->esd", grad_pair, w_in_wide).astype(jnp.bfloat16)
        returned = lax.optimization_barrier(returned)
        rows = returned.reshape(-1, D)[destination].reshape(group_rows, TOP, D)
        token_grad = jnp.sum(rows.astype(jnp.float32), axis=1).astype(jnp.bfloat16)
        sum_in = sum_in + lax.optimization_barrier(term_in.astype(jnp.bfloat16)).astype(jnp.float32)
        sum_down = sum_down + lax.optimization_barrier(term_down.astype(jnp.bfloat16)).astype(jnp.float32)
        return (sum_in, sum_down), token_grad

    start = (jnp.zeros((EXPERTS, D, 2 * FF), jnp.float32), jnp.zeros((EXPERTS, FF, D), jnp.float32))
    grouped = (
        tokens.reshape(N_DP, group_rows, D),
        cotangent.reshape(N_DP, group_rows, D),
        route_logits.reshape(N_DP, group_rows, TOP),
        expert_ids.reshape(N_DP, group_rows, TOP),
        slot_pos.reshape(N_DP, group_rows, TOP),
    )
    (grad_in, grad_down), token_grads = lax.scan(one_group, start, grouped)
    return token_grads.reshape(TOKENS, D), grad_in, grad_down
```

```python
import jax
import jax.numpy as jnp
from jax import lax
from jax.sharding import PartitionSpec as P

TOP = 2


def recompute(input_slots, w_in, hidden_width):
    gate_up = jnp.einsum("ksd,kdf->ksf", input_slots, w_in, preferred_element_type=jnp.float32)
    gate = gate_up[:, :, :hidden_width]
    upper = gate_up[:, :, hidden_width:]
    sigmoid_gate = jax.nn.sigmoid(gate)
    activated = gate * sigmoid_gate
    hidden = (activated * upper).astype(jnp.bfloat16)
    return (gate, upper, sigmoid_gate, activated, hidden)


def per_device(tokens, cotangent, route_logits, expert_ids, slot_pos, w_in, w_down):
    token_count, width = tokens.shape
    local_experts = w_in.shape[0]
    hidden_width = w_down.shape[1]
    n_expert = lax.axis_size("expert")
    n_dp = lax.axis_size("dp")
    experts_all = local_experts * n_expert
    capacity = 2 * TOP * token_count // experts_all
    first = jax.nn.sigmoid(route_logits[:, 0] - route_logits[:, 1])
    combine = jnp.stack([first, 1.0 - first], axis=1)
    scaled = (combine[:, :, None] * cotangent[:, None, :].astype(jnp.float32)).astype(jnp.bfloat16)
    destination = (expert_ids * capacity + slot_pos).reshape(-1)
    dest_in = (expert_ids * (2 * capacity) + slot_pos).reshape(-1)
    dest_all = jnp.concatenate([dest_in, dest_in + capacity])
    repeated = jnp.broadcast_to(tokens[:, None, :], (token_count, TOP, width)).reshape(-1, width)
    rows_all = jnp.concatenate([repeated, scaled.reshape(-1, width)], axis=0)
    empty = jnp.zeros((experts_all * 2 * capacity, width), jnp.bfloat16)
    send = empty.at[dest_all].set(rows_all).reshape(experts_all, 2, capacity, width)
    got = lax.all_to_all(send, "expert", split_axis=0, concat_axis=0, tiled=True)
    got = got.reshape(n_expert, local_experts, 2, capacity, width)
    got = jnp.transpose(got, (2, 1, 0, 3, 4)).reshape(2, local_experts, n_expert * capacity, width)
    input_slots, cotangent_slots = got[0], got[1]
    gate, upper, sigmoid_gate, activated, hidden = recompute(input_slots, w_in, hidden_width)
    grad_hidden = jnp.einsum(
        "ksd,kfd->ksf", cotangent_slots, w_down, preferred_element_type=jnp.float32
    )
    term_down = jnp.einsum(
        "ksf,ksd->kfd", hidden, cotangent_slots, preferred_element_type=jnp.float32
    )
    grad_gate = grad_hidden * upper * sigmoid_gate * (1.0 + gate * (1.0 - sigmoid_gate))
    grad_up = grad_hidden * activated
    grad_pair = jnp.concatenate([grad_gate, grad_up], axis=2).astype(jnp.bfloat16)
    term_in = jnp.einsum("ksd,ksf->kdf", input_slots, grad_pair, preferred_element_type=jnp.float32)
    returned = jnp.einsum(
        "ksf,kdf->ksd", grad_pair, w_in, preferred_element_type=jnp.float32
    ).astype(jnp.bfloat16)
    arrived = lax.all_to_all(returned, "expert", split_axis=1, concat_axis=0, tiled=True)
    rows = arrived.reshape(-1, width)[destination].reshape(token_count, TOP, width)
    input_grad = jnp.sum(rows.astype(jnp.float32), axis=1).astype(jnp.bfloat16)
    in_rows, in_cols = term_in.shape[1], term_in.shape[2]
    down_rows, down_cols = term_down.shape[1], term_down.shape[2]
    part_in = term_in.astype(jnp.bfloat16).reshape(local_experts, n_dp, -1)
    part_down = term_down.astype(jnp.bfloat16).reshape(local_experts, n_dp, -1)
    parts = jnp.transpose(jnp.concatenate([part_in, part_down], axis=2), (1, 0, 2))
    parts = parts.reshape(n_dp, -1, width)
    summed = lax.psum_scatter(parts, "dp", scatter_dimension=0, tiled=True).reshape(1, local_experts, -1)
    split = part_in.shape[2]
    grad_in = summed[0, :, :split].reshape(local_experts, in_rows // n_dp, in_cols).astype(jnp.float32)
    grad_down = summed[0, :, split:].reshape(local_experts, down_rows // n_dp, down_cols).astype(jnp.float32)
    return (input_grad, grad_in, grad_down)


def solution(mesh):
    in_specs = (
        P(("dp", "expert"), None),
        P(("dp", "expert"), None),
        P(("dp", "expert"), None),
        P(("dp", "expert"), None),
        P(("dp", "expert"), None),
        P("expert", None, None),
        P("expert", None, None),
    )
    out_specs = (P(("dp", "expert"), None), P("expert", "dp", None), P("expert", "dp", None))
    return jax.shard_map(
        per_device, mesh=mesh, in_specs=in_specs, out_specs=out_specs, check_vma=False
    )
```

```python
import jax
import jax.numpy as jnp
from jax import lax
from jax.sharding import PartitionSpec as P

TOP = 2


def recompute(input_slots, w_in, hidden_width):
    gate_up = jnp.einsum("ksd,kdf->ksf", input_slots, w_in, preferred_element_type=jnp.float32)
    gate = gate_up[:, :, :hidden_width]
    upper = gate_up[:, :, hidden_width:]
    sigmoid_gate = jax.nn.sigmoid(gate)
    activated = gate * sigmoid_gate
    hidden = (activated * upper).astype(jnp.bfloat16)
    return (gate, upper, sigmoid_gate, activated, hidden)


def per_device(tokens, cotangent, route_logits, expert_ids, slot_pos, w_in, w_down):
    token_count, width = tokens.shape
    local_experts = w_in.shape[0]
    hidden_width = w_down.shape[1]
    n_expert = lax.axis_size("expert")
    n_dp = lax.axis_size("dp")
    experts_all = local_experts * n_expert
    capacity = 2 * TOP * token_count // experts_all
    first = jax.nn.sigmoid(route_logits[:, 0] - route_logits[:, 1])
    combine = jnp.stack([first, 1.0 - first], axis=1)
    scaled = (combine[:, :, None] * cotangent[:, None, :].astype(jnp.float32)).astype(jnp.bfloat16)
    destination = (expert_ids * capacity + slot_pos).reshape(-1)
    target = expert_ids * (2 * capacity) + slot_pos
    sources = jnp.concatenate([tokens, scaled.reshape(-1, width)], axis=0)
    first_row = jnp.concatenate([target[:, 0], target.reshape(-1) + capacity])
    second_row = jnp.concatenate([target[:, 1], jnp.full((TOP * token_count,), -1, jnp.int32)])
    buffer_row = lax.broadcasted_iota(jnp.int32, (experts_all * 2 * capacity, sources.shape[0]), 0)
    picks = ((buffer_row == first_row[None, :]) | (buffer_row == second_row[None, :])).astype(jnp.bfloat16)
    send = jnp.dot(picks, sources, preferred_element_type=jnp.float32).astype(jnp.bfloat16)
    send = send.reshape(experts_all, 2, capacity, width)
    got = lax.all_to_all(send, "expert", split_axis=0, concat_axis=0, tiled=True)
    got = got.reshape(n_expert, local_experts, 2, capacity, width)
    got = jnp.transpose(got, (2, 1, 0, 3, 4)).reshape(2, local_experts, n_expert * capacity, width)
    input_slots, cotangent_slots = got[0], got[1]
    gate, upper, sigmoid_gate, activated, hidden = recompute(input_slots, w_in, hidden_width)
    grad_hidden = jnp.einsum(
        "ksd,kfd->ksf", cotangent_slots, w_down, preferred_element_type=jnp.float32
    )
    term_down = jnp.einsum(
        "ksf,ksd->kfd", hidden, cotangent_slots, preferred_element_type=jnp.float32
    )
    grad_gate = grad_hidden * upper * sigmoid_gate * (1.0 + gate * (1.0 - sigmoid_gate))
    grad_up = grad_hidden * activated
    grad_pair = jnp.concatenate([grad_gate, grad_up], axis=2).astype(jnp.bfloat16)
    term_in = jnp.einsum("ksd,ksf->kdf", input_slots, grad_pair, preferred_element_type=jnp.float32)
    returned = jnp.einsum(
        "ksf,kdf->ksd", grad_pair, w_in, preferred_element_type=jnp.float32
    ).astype(jnp.bfloat16)
    arrived = lax.all_to_all(returned, "expert", split_axis=1, concat_axis=0, tiled=True)
    rows = arrived.reshape(-1, width)[destination].reshape(token_count, TOP, width)
    input_grad = jnp.sum(rows.astype(jnp.float32), axis=1).astype(jnp.bfloat16)
    in_rows, in_cols = term_in.shape[1], term_in.shape[2]
    down_rows, down_cols = term_down.shape[1], term_down.shape[2]
    part_in = term_in.astype(jnp.bfloat16).reshape(local_experts, n_dp, in_rows // n_dp, in_cols)
    down_flat = (down_rows // n_dp) * down_cols // in_cols
    part_down = term_down.astype(jnp.bfloat16).reshape(local_experts, n_dp, down_flat, in_cols)
    parts = jnp.concatenate([part_in, part_down], axis=2).reshape(local_experts, -1, in_cols)
    summed = lax.psum_scatter(parts, "dp", scatter_dimension=1, tiled=True)
    grad_in = summed[:, : in_rows // n_dp].astype(jnp.float32)
    grad_down = summed[:, in_rows // n_dp :].reshape(local_experts, down_rows // n_dp, down_cols).astype(jnp.float32)
    return (input_grad, grad_in, grad_down)


def solution(mesh):
    in_specs = (
        P(("dp", "expert"), None),
        P(("dp", "expert"), None),
        P(("dp", "expert"), None),
        P(("dp", "expert"), None),
        P(("dp", "expert"), None),
        P("expert", None, None),
        P("expert", None, None),
    )
    out_specs = (P(("dp", "expert"), None), P("expert", "dp", None), P("expert", "dp", None))
    return jax.shard_map(
        per_device, mesh=mesh, in_specs=in_specs, out_specs=out_specs, check_vma=False
    )
```

```python
import jax
import jax.numpy as jnp
from jax import lax
from jax.sharding import PartitionSpec as P

TOP = 2


def recompute(input_slots, w_in, hidden_width):
    gate_up = jnp.einsum("ksd,kdf->ksf", input_slots, w_in, preferred_element_type=jnp.float32)
    gate = gate_up[:, :, :hidden_width]
    upper = gate_up[:, :, hidden_width:]
    sigmoid_gate = jax.nn.sigmoid(gate)
    activated = gate * sigmoid_gate
    hidden = (activated * upper).astype(jnp.bfloat16)
    return (gate, upper, sigmoid_gate, activated, hidden)


def per_device(tokens, cotangent, route_logits, expert_ids, slot_pos, w_in, w_down):
    token_count, width = tokens.shape
    local_experts = w_in.shape[0]
    hidden_width = w_down.shape[1]
    n_expert = lax.axis_size("expert")
    n_z, n_core = lax.axis_size("dz"), lax.axis_size("dc")
    n_dp = n_z * n_core
    experts_all = local_experts * n_expert
    capacity = 2 * TOP * token_count // experts_all
    first = jax.nn.sigmoid(route_logits[:, 0] - route_logits[:, 1])
    combine = jnp.stack([first, 1.0 - first], axis=1)
    scaled = (combine[:, :, None] * cotangent[:, None, :].astype(jnp.float32)).astype(jnp.bfloat16)
    destination = (expert_ids * capacity + slot_pos).reshape(-1)
    target = expert_ids * (2 * capacity) + slot_pos
    sources = jnp.concatenate([tokens, scaled.reshape(-1, width)], axis=0)
    first_row = jnp.concatenate([target[:, 0], target.reshape(-1) + capacity])
    second_row = jnp.concatenate([target[:, 1], jnp.full((TOP * token_count,), -1, jnp.int32)])
    buffer_row = lax.broadcasted_iota(jnp.int32, (experts_all * 2 * capacity, sources.shape[0]), 0)
    picks = ((buffer_row == first_row[None, :]) | (buffer_row == second_row[None, :])).astype(jnp.bfloat16)
    send = jnp.dot(picks, sources, preferred_element_type=jnp.float32).astype(jnp.bfloat16)
    send = send.reshape(experts_all, 2, capacity, width)
    got = lax.all_to_all(send, "expert", split_axis=0, concat_axis=0, tiled=True)
    got = got.reshape(n_expert, local_experts, 2, capacity, width)
    got = jnp.transpose(got, (2, 1, 0, 3, 4)).reshape(2, local_experts, n_expert * capacity, width)
    input_slots, cotangent_slots = got[0], got[1]
    gate, upper, sigmoid_gate, activated, hidden = recompute(input_slots, w_in, hidden_width)
    grad_hidden = jnp.einsum(
        "ksd,kfd->ksf", cotangent_slots, w_down, preferred_element_type=jnp.float32
    )
    term_down = jnp.einsum(
        "ksf,ksd->kfd", hidden, cotangent_slots, preferred_element_type=jnp.float32
    )
    grad_gate = grad_hidden * upper * sigmoid_gate * (1.0 + gate * (1.0 - sigmoid_gate))
    grad_up = grad_hidden * activated
    grad_pair = jnp.concatenate([grad_gate, grad_up], axis=2).astype(jnp.bfloat16)
    term_in = jnp.einsum("ksd,ksf->kdf", input_slots, grad_pair, preferred_element_type=jnp.float32)
    returned = jnp.einsum(
        "ksf,kdf->ksd", grad_pair, w_in, preferred_element_type=jnp.float32
    ).astype(jnp.bfloat16)
    arrived = lax.all_to_all(returned, "expert", split_axis=1, concat_axis=0, tiled=True)
    rows = arrived.reshape(-1, width)[destination].reshape(token_count, TOP, width)
    input_grad = jnp.sum(rows.astype(jnp.float32), axis=1).astype(jnp.bfloat16)
    in_rows, in_cols = term_in.shape[1], term_in.shape[2]
    down_rows, down_cols = term_down.shape[1], term_down.shape[2]
    part_in = term_in.astype(jnp.bfloat16).reshape(local_experts, n_dp, in_rows // n_dp, in_cols)
    down_flat = (down_rows // n_dp) * down_cols // in_cols
    part_down = term_down.astype(jnp.bfloat16).reshape(local_experts, n_dp, down_flat, in_cols)
    parts = jnp.concatenate([part_in, part_down], axis=2)
    parts = parts.reshape(local_experts, n_z, n_core, -1, in_cols)
    parts = jnp.transpose(parts, (0, 2, 1, 3, 4)).reshape(local_experts, -1, in_cols)
    summed = lax.psum_scatter(parts, "dc", scatter_dimension=1, tiled=True)
    summed = lax.psum_scatter(summed, "dz", scatter_dimension=1, tiled=True)
    grad_in = summed[:, : in_rows // n_dp].astype(jnp.float32)
    grad_down = summed[:, in_rows // n_dp :].reshape(local_experts, down_rows // n_dp, down_cols).astype(jnp.float32)
    return (input_grad, grad_in, grad_down)


def solution(mesh):
    n_dp = mesh.shape["dp"]
    n_z = n_dp // 2
    split_mesh = jax.sharding.Mesh(
        mesh.devices.reshape(n_z, n_dp // n_z, mesh.shape["expert"]), ("dz", "dc", "expert")
    )
    dp = ("dz", "dc")
    in_specs = (
        P((*dp, "expert"), None),
        P((*dp, "expert"), None),
        P((*dp, "expert"), None),
        P((*dp, "expert"), None),
        P((*dp, "expert"), None),
        P("expert", None, None),
        P("expert", None, None),
    )
    out_specs = (P((*dp, "expert"), None), P("expert", dp, None), P("expert", dp, None))
    return jax.shard_map(
        per_device, mesh=split_mesh, in_specs=in_specs, out_specs=out_specs, check_vma=False
    )
```

```python
import jax
import jax.numpy as jnp
from jax import lax
from jax.sharding import PartitionSpec as P

TOP = 2


def recompute(input_slots, w_in, hidden_width):
    gate_up = jnp.einsum("ksd,kdf->ksf", input_slots, w_in, preferred_element_type=jnp.float32)
    gate = gate_up[:, :, :hidden_width]
    upper = gate_up[:, :, hidden_width:]
    sigmoid_gate = jax.nn.sigmoid(gate)
    activated = gate * sigmoid_gate
    hidden = (activated * upper).astype(jnp.bfloat16)
    return (gate, upper, sigmoid_gate, activated, hidden)


def per_device(tokens, cotangent, route_logits, expert_ids, slot_pos, w_in, w_down):
    token_count, width = tokens.shape
    local_experts = w_in.shape[0]
    hidden_width = w_down.shape[1]
    n_expert = lax.axis_size("expert")
    n_dp = lax.axis_size("dp")
    experts_all = local_experts * n_expert
    capacity = 2 * TOP * token_count // experts_all
    first = jax.nn.sigmoid(route_logits[:, 0] - route_logits[:, 1])
    combine = (first, 1.0 - first)
    cotangent_wide = cotangent.astype(jnp.float32)
    destination = (expert_ids * capacity + slot_pos).reshape(-1)
    target = expert_ids * (2 * capacity) + slot_pos
    buffer_row = lax.broadcasted_iota(jnp.int32, (experts_all * 2 * capacity, token_count), 0)
    picks = []
    for k in range(TOP):
        picks.append((buffer_row == target[None, :, k]).astype(jnp.bfloat16))
    token_picks = picks[0] + picks[1]
    send = jnp.dot(token_picks, tokens, preferred_element_type=jnp.float32)
    for k in range(TOP):
        scaled = (combine[k][:, None] * cotangent_wide).astype(jnp.bfloat16)
        shifted = (buffer_row == target[None, :, k] + capacity).astype(jnp.bfloat16)
        send = send + jnp.dot(shifted, scaled, preferred_element_type=jnp.float32)
    send = send.astype(jnp.bfloat16).reshape(experts_all, 2, capacity, width)
    got = lax.all_to_all(send, "expert", split_axis=0, concat_axis=0, tiled=True)
    got = got.reshape(n_expert, local_experts, 2, capacity, width)
    got = jnp.transpose(got, (2, 1, 0, 3, 4)).reshape(2, local_experts, n_expert * capacity, width)
    input_slots, cotangent_slots = got[0], got[1]
    gate, upper, sigmoid_gate, activated, hidden = recompute(input_slots, w_in, hidden_width)
    grad_hidden = jnp.einsum(
        "ksd,kfd->ksf", cotangent_slots, w_down, preferred_element_type=jnp.float32
    )
    term_down = jnp.einsum(
        "ksf,ksd->kfd", hidden, cotangent_slots, preferred_element_type=jnp.float32
    )
    grad_gate = grad_hidden * upper * sigmoid_gate * (1.0 + gate * (1.0 - sigmoid_gate))
    grad_up = grad_hidden * activated
    grad_pair = jnp.concatenate([grad_gate, grad_up], axis=2).astype(jnp.bfloat16)
    term_in = jnp.einsum("ksd,ksf->kdf", input_slots, grad_pair, preferred_element_type=jnp.float32)
    returned = jnp.einsum(
        "ksf,kdf->ksd", grad_pair, w_in, preferred_element_type=jnp.float32
    ).astype(jnp.bfloat16)
    arrived = lax.all_to_all(returned, "expert", split_axis=1, concat_axis=0, tiled=True)
    rows = arrived.reshape(-1, width)[destination].reshape(token_count, TOP, width)
    input_grad = jnp.sum(rows.astype(jnp.float32), axis=1).astype(jnp.bfloat16)
    in_rows, in_cols = term_in.shape[1], term_in.shape[2]
    down_rows, down_cols = term_down.shape[1], term_down.shape[2]
    part_in = term_in.astype(jnp.bfloat16).reshape(local_experts, n_dp, in_rows // n_dp, in_cols)
    down_flat = (down_rows // n_dp) * down_cols // in_cols
    part_down = term_down.astype(jnp.bfloat16).reshape(local_experts, n_dp, down_flat, in_cols)
    parts = jnp.concatenate([part_in, part_down], axis=2).reshape(local_experts, -1, in_cols)
    summed = lax.psum_scatter(parts, "dp", scatter_dimension=1, tiled=True)
    grad_in = summed[:, : in_rows // n_dp].astype(jnp.float32)
    grad_down = summed[:, in_rows // n_dp :].reshape(local_experts, down_rows // n_dp, down_cols).astype(jnp.float32)
    return (input_grad, grad_in, grad_down)


def solution(mesh):
    in_specs = (
        P(("dp", "expert"), None),
        P(("dp", "expert"), None),
        P(("dp", "expert"), None),
        P(("dp", "expert"), None),
        P(("dp", "expert"), None),
        P("expert", None, None),
        P("expert", None, None),
    )
    out_specs = (P(("dp", "expert"), None), P("expert", "dp", None), P("expert", "dp", None))
    return jax.shard_map(
        per_device, mesh=mesh, in_specs=in_specs, out_specs=out_specs, check_vma=False
    )
```

```python
import jax
import jax.numpy as jnp
from jax import lax
from jax.sharding import PartitionSpec as P

TOP = 2


def recompute(input_slots, w_in, hidden_width):
    gate_up = jnp.einsum("ksd,kdf->ksf", input_slots, w_in, preferred_element_type=jnp.float32)
    gate = gate_up[:, :, :hidden_width]
    upper = gate_up[:, :, hidden_width:]
    sigmoid_gate = jax.nn.sigmoid(gate)
    activated = gate * sigmoid_gate
    hidden = (activated * upper).astype(jnp.bfloat16)
    return (gate, upper, sigmoid_gate, activated, hidden)


def per_device(tokens, cotangent, route_logits, expert_ids, slot_pos, w_in, w_down):
    token_count, width = tokens.shape
    local_experts = w_in.shape[0]
    hidden_width = w_down.shape[1]
    n_expert = lax.axis_size("expert")
    n_dp = lax.axis_size("dp")
    experts_all = local_experts * n_expert
    capacity = 2 * TOP * token_count // experts_all
    first = jax.nn.sigmoid(route_logits[:, 0] - route_logits[:, 1])
    combine = (first, 1.0 - first)
    cotangent_wide = cotangent.astype(jnp.float32)
    destination = (expert_ids * capacity + slot_pos).reshape(-1)
    target = expert_ids * (2 * capacity) + slot_pos
    buffer_row = lax.broadcasted_iota(jnp.int32, (experts_all * 2 * capacity, token_count), 0)
    picks = []
    for k in range(TOP):
        picks.append((buffer_row == target[None, :, k]).astype(jnp.bfloat16))
    token_picks = picks[0] + picks[1]
    send = jnp.dot(token_picks, tokens, preferred_element_type=jnp.float32)
    for k in range(TOP):
        scaled = (combine[k][:, None] * cotangent_wide).astype(jnp.bfloat16)
        shifted = (buffer_row == target[None, :, k] + capacity).astype(jnp.bfloat16)
        send = send + jnp.dot(shifted, scaled, preferred_element_type=jnp.float32)
    send = send.astype(jnp.bfloat16).reshape(experts_all, 2, capacity, width)
    got = lax.all_to_all(send, "expert", split_axis=0, concat_axis=0, tiled=True)
    got = got.reshape(n_expert, local_experts, 2, capacity, width)
    got = jnp.transpose(got, (2, 1, 0, 3, 4)).reshape(2, local_experts, n_expert * capacity, width)
    input_slots, cotangent_slots = got[0], got[1]
    gate, upper, sigmoid_gate, activated, hidden = recompute(input_slots, w_in, hidden_width)
    grad_hidden = jnp.einsum(
        "ksd,kfd->ksf", cotangent_slots, w_down, preferred_element_type=jnp.float32
    )
    term_down = jnp.einsum(
        "ksf,ksd->kfd", hidden, cotangent_slots, preferred_element_type=jnp.float32
    )
    grad_gate = grad_hidden * upper * sigmoid_gate * (1.0 + gate * (1.0 - sigmoid_gate))
    grad_up = grad_hidden * activated
    grad_pair = jnp.concatenate([grad_gate, grad_up], axis=2).astype(jnp.bfloat16)
    term_in = jnp.einsum("ksd,ksf->kdf", input_slots, grad_pair, preferred_element_type=jnp.float32)
    returned = jnp.einsum(
        "ksf,kdf->ksd", grad_pair, w_in, preferred_element_type=jnp.float32
    ).astype(jnp.bfloat16)
    arrived = lax.all_to_all(returned, "expert", split_axis=1, concat_axis=0, tiled=True)
    rows = arrived.reshape(-1, width)[destination].reshape(token_count, TOP, width)
    input_grad = jnp.sum(rows.astype(jnp.float32), axis=1).astype(jnp.bfloat16)
    in_rows, in_cols = term_in.shape[1], term_in.shape[2]
    down_rows, down_cols = term_down.shape[1], term_down.shape[2]
    rows_q = down_rows // n_dp
    main = rows_q * down_cols // in_cols
    spare = in_cols - down_cols
    part_in = term_in.astype(jnp.bfloat16).reshape(local_experts, n_dp, in_rows // n_dp, in_cols)
    part_down = term_down.astype(jnp.bfloat16).reshape(local_experts, n_dp, rows_q, down_cols)
    pieces = [part_down[:, :, main:, c : c + spare] for c in range(0, down_cols, spare)]
    packed = jnp.concatenate([part_down[:, :, :main], jnp.concatenate(pieces, axis=2)], axis=3)
    parts = jnp.concatenate([part_in, packed], axis=2).reshape(local_experts, -1, in_cols)
    summed = lax.psum_scatter(parts, "dp", scatter_dimension=1, tiled=True)
    grad_in = summed[:, : in_rows // n_dp].astype(jnp.float32)
    got_down = summed[:, in_rows // n_dp :]
    rest = rows_q - main
    tail = [got_down[:, i * rest : (i + 1) * rest, down_cols:] for i in range(down_cols // spare)]
    grad_down = jnp.concatenate([got_down[:, :, :down_cols], jnp.concatenate(tail, axis=2)], axis=1)
    grad_down = grad_down.astype(jnp.float32)
    return (input_grad, grad_in, grad_down)


def solution(mesh):
    in_specs = (
        P(("dp", "expert"), None),
        P(("dp", "expert"), None),
        P(("dp", "expert"), None),
        P(("dp", "expert"), None),
        P(("dp", "expert"), None),
        P("expert", None, None),
        P("expert", None, None),
    )
    out_specs = (P(("dp", "expert"), None), P("expert", "dp", None), P("expert", "dp", None))
    return jax.shard_map(
        per_device, mesh=mesh, in_specs=in_specs, out_specs=out_specs, check_vma=False
    )
```

```python
import jax
import jax.numpy as jnp
from jax import lax
from jax.sharding import PartitionSpec as P

TOP = 2


def recompute(input_slots, w_in, hidden_width):
    gate_up = jnp.einsum("ksd,kdf->ksf", input_slots, w_in, preferred_element_type=jnp.float32)
    gate = gate_up[:, :, :hidden_width]
    upper = gate_up[:, :, hidden_width:]
    sigmoid_gate = jax.nn.sigmoid(gate)
    activated = gate * sigmoid_gate
    hidden = (activated * upper).astype(jnp.bfloat16)
    return (gate, upper, sigmoid_gate, activated, hidden)


def per_device(tokens, cotangent, route_logits, expert_ids, slot_pos, w_in, w_down):
    token_count, width = tokens.shape
    local_experts = w_in.shape[0]
    hidden_width = w_down.shape[1]
    n_expert = lax.axis_size("expert")
    n_dp = lax.axis_size("dp")
    experts_all = local_experts * n_expert
    capacity = 2 * TOP * token_count // experts_all
    first = jax.nn.sigmoid(route_logits[:, 0] - route_logits[:, 1])
    combine = (first, 1.0 - first)
    cotangent_wide = cotangent.astype(jnp.float32)
    destination = (expert_ids * capacity + slot_pos).reshape(-1)
    target = expert_ids * (2 * capacity) + slot_pos
    sources = [tokens]
    first_row, second_row = [target[:, 0]], [target[:, 1]]
    for k in range(TOP):
        sources.append((combine[k][:, None] * cotangent_wide).astype(jnp.bfloat16))
        first_row.append(target[:, k] + capacity)
        second_row.append(jnp.full((token_count,), -1, jnp.int32))
    sources = jnp.concatenate(sources, axis=0)
    first_row = jnp.concatenate(first_row)
    second_row = jnp.concatenate(second_row)
    buffer_row = lax.broadcasted_iota(jnp.int32, (experts_all * 2 * capacity, sources.shape[0]), 0)
    picks = ((buffer_row == first_row[None, :]) | (buffer_row == second_row[None, :])).astype(jnp.bfloat16)
    send = jnp.dot(picks, sources, preferred_element_type=jnp.float32)
    send = send.astype(jnp.bfloat16).reshape(experts_all, 2, capacity, width)
    got = lax.all_to_all(send, "expert", split_axis=0, concat_axis=0, tiled=True)
    got = got.reshape(n_expert, local_experts, 2, capacity, width)
    got = jnp.transpose(got, (2, 1, 0, 3, 4)).reshape(2, local_experts, n_expert * capacity, width)
    input_slots, cotangent_slots = got[0], got[1]
    gate, upper, sigmoid_gate, activated, hidden = recompute(input_slots, w_in, hidden_width)
    grad_hidden = jnp.einsum(
        "ksd,kfd->ksf", cotangent_slots, w_down, preferred_element_type=jnp.float32
    )
    term_down = jnp.einsum(
        "ksf,ksd->kfd", hidden, cotangent_slots, preferred_element_type=jnp.float32
    )
    grad_gate = grad_hidden * upper * sigmoid_gate * (1.0 + gate * (1.0 - sigmoid_gate))
    grad_up = grad_hidden * activated
    grad_pair = jnp.concatenate([grad_gate, grad_up], axis=2).astype(jnp.bfloat16)
    term_in = jnp.einsum("ksd,ksf->kdf", input_slots, grad_pair, preferred_element_type=jnp.float32)
    returned = jnp.einsum(
        "ksf,kdf->ksd", grad_pair, w_in, preferred_element_type=jnp.float32
    ).astype(jnp.bfloat16)
    arrived = lax.all_to_all(returned, "expert", split_axis=1, concat_axis=0, tiled=True)
    rows = arrived.reshape(-1, width)[destination].reshape(token_count, TOP, width)
    input_grad = jnp.sum(rows.astype(jnp.float32), axis=1).astype(jnp.bfloat16)
    in_rows, in_cols = term_in.shape[1], term_in.shape[2]
    down_rows, down_cols = term_down.shape[1], term_down.shape[2]
    rows_q = down_rows // n_dp
    main = rows_q * down_cols // in_cols
    spare = in_cols - down_cols
    part_in = term_in.astype(jnp.bfloat16).reshape(local_experts, n_dp, in_rows // n_dp, in_cols)
    part_down = term_down.astype(jnp.bfloat16).reshape(local_experts, n_dp, rows_q, down_cols)
    pieces = [part_down[:, :, main:, c : c + spare] for c in range(0, down_cols, spare)]
    packed = jnp.concatenate([part_down[:, :, :main], jnp.concatenate(pieces, axis=2)], axis=3)
    parts = jnp.concatenate([part_in, packed], axis=2).reshape(local_experts, -1, in_cols)
    summed = lax.psum_scatter(parts, "dp", scatter_dimension=1, tiled=True)
    grad_in = summed[:, : in_rows // n_dp].astype(jnp.float32)
    got_down = summed[:, in_rows // n_dp :]
    rest = rows_q - main
    tail = [got_down[:, i * rest : (i + 1) * rest, down_cols:] for i in range(down_cols // spare)]
    grad_down = jnp.concatenate([got_down[:, :, :down_cols], jnp.concatenate(tail, axis=2)], axis=1)
    grad_down = grad_down.astype(jnp.float32)
    return (input_grad, grad_in, grad_down)


def solution(mesh):
    in_specs = (
        P(("dp", "expert"), None),
        P(("dp", "expert"), None),
        P(("dp", "expert"), None),
        P(("dp", "expert"), None),
        P(("dp", "expert"), None),
        P("expert", None, None),
        P("expert", None, None),
    )
    out_specs = (P(("dp", "expert"), None), P("expert", "dp", None), P("expert", "dp", None))
    return jax.shard_map(
        per_device, mesh=mesh, in_specs=in_specs, out_specs=out_specs, check_vma=False
    )
```

```python
import jax
import jax.numpy as jnp
from jax import lax
from jax.sharding import PartitionSpec as P

TOP = 2


def recompute(input_slots, w_in, hidden_width):
    gate = jnp.einsum(
        "ksd,kdf->ksf", input_slots, w_in[:, :, :hidden_width], preferred_element_type=jnp.float32
    )
    upper = jnp.einsum(
        "ksd,kdf->ksf", input_slots, w_in[:, :, hidden_width:], preferred_element_type=jnp.float32
    )
    sigmoid_gate = jax.nn.sigmoid(gate)
    activated = gate * sigmoid_gate
    hidden = (activated * upper).astype(jnp.bfloat16)
    return (gate, upper, sigmoid_gate, activated, hidden)


def per_device(tokens, cotangent, route_logits, expert_ids, slot_pos, w_in, w_down):
    token_count, width = tokens.shape
    local_experts = w_in.shape[0]
    hidden_width = w_down.shape[1]
    n_expert = lax.axis_size("expert")
    n_dp = lax.axis_size("dp")
    experts_all = local_experts * n_expert
    capacity = 2 * TOP * token_count // experts_all
    first = jax.nn.sigmoid(route_logits[:, 0] - route_logits[:, 1])
    combine = (first, 1.0 - first)
    cotangent_wide = cotangent.astype(jnp.float32)
    destination = (expert_ids * capacity + slot_pos).reshape(-1)
    target = expert_ids * (2 * capacity) + slot_pos
    buffer_row = lax.broadcasted_iota(jnp.int32, (experts_all * 2 * capacity, token_count), 0)
    picks = []
    for k in range(TOP):
        picks.append((buffer_row == target[None, :, k]).astype(jnp.bfloat16))
    token_picks = picks[0] + picks[1]
    send = jnp.dot(token_picks, tokens, preferred_element_type=jnp.float32)
    for k in range(TOP):
        scaled = (combine[k][:, None] * cotangent_wide).astype(jnp.bfloat16)
        shifted = (buffer_row == target[None, :, k] + capacity).astype(jnp.bfloat16)
        send = send + jnp.dot(shifted, scaled, preferred_element_type=jnp.float32)
    send = send.astype(jnp.bfloat16).reshape(experts_all, 2, capacity, width)
    got = lax.all_to_all(send, "expert", split_axis=0, concat_axis=0, tiled=True)
    got = got.reshape(n_expert, local_experts, 2, capacity, width)
    got = jnp.transpose(got, (2, 1, 0, 3, 4)).reshape(2, local_experts, n_expert * capacity, width)
    input_slots, cotangent_slots = got[0], got[1]
    gate, upper, sigmoid_gate, activated, hidden = recompute(input_slots, w_in, hidden_width)
    grad_hidden = jnp.einsum(
        "ksd,kfd->ksf", cotangent_slots, w_down, preferred_element_type=jnp.float32
    )
    term_down = jnp.einsum(
        "ksf,ksd->kfd", hidden, cotangent_slots, preferred_element_type=jnp.float32
    )
    grad_gate = grad_hidden * upper * sigmoid_gate * (1.0 + gate * (1.0 - sigmoid_gate))
    grad_up = grad_hidden * activated
    grad_pair = jnp.concatenate([grad_gate, grad_up], axis=2).astype(jnp.bfloat16)
    term_in = jnp.einsum("ksd,ksf->kdf", input_slots, grad_pair, preferred_element_type=jnp.float32)
    returned = jnp.einsum(
        "ksf,kdf->ksd", grad_pair, w_in, preferred_element_type=jnp.float32
    ).astype(jnp.bfloat16)
    arrived = lax.all_to_all(returned, "expert", split_axis=1, concat_axis=0, tiled=True)
    rows = arrived.reshape(-1, width)[destination].reshape(token_count, TOP, width)
    input_grad = jnp.sum(rows.astype(jnp.float32), axis=1).astype(jnp.bfloat16)
    in_rows, in_cols = term_in.shape[1], term_in.shape[2]
    down_rows, down_cols = term_down.shape[1], term_down.shape[2]
    rows_q = down_rows // n_dp
    main = rows_q * down_cols // in_cols
    spare = in_cols - down_cols
    part_in = term_in.astype(jnp.bfloat16).reshape(local_experts, n_dp, in_rows // n_dp, in_cols)
    part_down = term_down.astype(jnp.bfloat16).reshape(local_experts, n_dp, rows_q, down_cols)
    pieces = [part_down[:, :, main:, c : c + spare] for c in range(0, down_cols, spare)]
    packed = jnp.concatenate([part_down[:, :, :main], jnp.concatenate(pieces, axis=2)], axis=3)
    parts = jnp.concatenate([part_in, packed], axis=2).reshape(local_experts, -1, in_cols)
    summed = lax.psum_scatter(parts, "dp", scatter_dimension=1, tiled=True)
    grad_in = summed[:, : in_rows // n_dp].astype(jnp.float32)
    got_down = summed[:, in_rows // n_dp :]
    rest = rows_q - main
    tail = [got_down[:, i * rest : (i + 1) * rest, down_cols:] for i in range(down_cols // spare)]
    grad_down = jnp.concatenate([got_down[:, :, :down_cols], jnp.concatenate(tail, axis=2)], axis=1)
    grad_down = grad_down.astype(jnp.float32)
    return (input_grad, grad_in, grad_down)


def solution(mesh):
    in_specs = (
        P(("dp", "expert"), None),
        P(("dp", "expert"), None),
        P(("dp", "expert"), None),
        P(("dp", "expert"), None),
        P(("dp", "expert"), None),
        P("expert", None, None),
        P("expert", None, None),
    )
    out_specs = (P(("dp", "expert"), None), P("expert", "dp", None), P("expert", "dp", None))
    return jax.shard_map(
        per_device, mesh=mesh, in_specs=in_specs, out_specs=out_specs, check_vma=False
    )
```

```python
import jax
import jax.numpy as jnp
from jax import lax
from jax.sharding import PartitionSpec as P

TOP = 2


def recompute(input_slots, w_in, hidden_width):
    gate = jnp.einsum(
        "ksd,kdf->ksf", input_slots, w_in[:, :, :hidden_width], preferred_element_type=jnp.float32
    )
    upper = jnp.einsum(
        "ksd,kdf->ksf", input_slots, w_in[:, :, hidden_width:], preferred_element_type=jnp.float32
    )
    sigmoid_gate = jax.nn.sigmoid(gate)
    activated = gate * sigmoid_gate
    hidden = (activated * upper).astype(jnp.bfloat16)
    return (gate, upper, sigmoid_gate, activated, hidden)


def per_device(tokens, cotangent, route_logits, expert_ids, slot_pos, w_in, w_down):
    token_count, width = tokens.shape
    local_experts = w_in.shape[0]
    hidden_width = w_down.shape[1]
    n_expert = lax.axis_size("expert")
    n_dp = lax.axis_size("dp")
    experts_all = local_experts * n_expert
    capacity = 2 * TOP * token_count // experts_all
    first = jax.nn.sigmoid(route_logits[:, 0] - route_logits[:, 1])
    combine = (first, 1.0 - first)
    cotangent_wide = cotangent.astype(jnp.float32)
    destination = (expert_ids * capacity + slot_pos).reshape(-1)
    target = expert_ids * capacity + slot_pos
    buffer_row = lax.broadcasted_iota(jnp.int32, (experts_all * capacity, token_count), 0)
    picks = [(buffer_row == target[None, :, k]).astype(jnp.bfloat16) for k in range(TOP)]
    send_tokens = jnp.dot(picks[0] + picks[1], tokens, preferred_element_type=jnp.float32)
    send_scaled = 0.0
    for k in range(TOP):
        scaled = (combine[k][:, None] * cotangent_wide).astype(jnp.bfloat16)
        send_scaled = send_scaled + jnp.dot(picks[k], scaled, preferred_element_type=jnp.float32)
    send = jnp.stack([send_tokens, send_scaled]).astype(jnp.bfloat16)
    send = send.reshape(2, experts_all, capacity, width)
    got = lax.all_to_all(send, "expert", split_axis=1, concat_axis=1, tiled=True)
    got = got.reshape(2, n_expert, local_experts, capacity, width)
    got = jnp.swapaxes(got, 1, 2).reshape(2, local_experts, n_expert * capacity, width)
    input_slots, cotangent_slots = got[0], got[1]
    gate, upper, sigmoid_gate, activated, hidden = recompute(input_slots, w_in, hidden_width)
    grad_hidden = jnp.einsum(
        "ksd,kfd->ksf", cotangent_slots, w_down, preferred_element_type=jnp.float32
    )
    term_down = jnp.einsum(
        "ksf,ksd->kfd", hidden, cotangent_slots, preferred_element_type=jnp.float32
    )
    grad_gate = grad_hidden * upper * sigmoid_gate * (1.0 + gate * (1.0 - sigmoid_gate))
    grad_up = grad_hidden * activated
    grad_pair = jnp.concatenate([grad_gate, grad_up], axis=2).astype(jnp.bfloat16)
    term_in = jnp.einsum("ksd,ksf->kdf", input_slots, grad_pair, preferred_element_type=jnp.float32)
    returned = jnp.einsum(
        "ksf,kdf->ksd", grad_pair, w_in, preferred_element_type=jnp.float32
    ).astype(jnp.bfloat16)
    arrived = lax.all_to_all(returned, "expert", split_axis=1, concat_axis=0, tiled=True)
    rows = arrived.reshape(-1, width)[destination].reshape(token_count, TOP, width)
    input_grad = jnp.sum(rows.astype(jnp.float32), axis=1).astype(jnp.bfloat16)
    in_rows, in_cols = term_in.shape[1], term_in.shape[2]
    down_rows, down_cols = term_down.shape[1], term_down.shape[2]
    rows_q = down_rows // n_dp
    main = rows_q * down_cols // in_cols
    spare = in_cols - down_cols
    part_in = term_in.astype(jnp.bfloat16).reshape(local_experts, n_dp, in_rows // n_dp, in_cols)
    part_down = term_down.astype(jnp.bfloat16).reshape(local_experts, n_dp, rows_q, down_cols)
    pieces = [part_down[:, :, main:, c : c + spare] for c in range(0, down_cols, spare)]
    packed = jnp.concatenate([part_down[:, :, :main], jnp.concatenate(pieces, axis=2)], axis=3)
    parts = jnp.concatenate([part_in, packed], axis=2).reshape(local_experts, -1, in_cols)
    summed = lax.psum_scatter(parts, "dp", scatter_dimension=1, tiled=True)
    grad_in = summed[:, : in_rows // n_dp].astype(jnp.float32)
    got_down = summed[:, in_rows // n_dp :]
    rest = rows_q - main
    tail = [got_down[:, i * rest : (i + 1) * rest, down_cols:] for i in range(down_cols // spare)]
    grad_down = jnp.concatenate([got_down[:, :, :down_cols], jnp.concatenate(tail, axis=2)], axis=1)
    grad_down = grad_down.astype(jnp.float32)
    return (input_grad, grad_in, grad_down)


def solution(mesh):
    in_specs = (
        P(("dp", "expert"), None),
        P(("dp", "expert"), None),
        P(("dp", "expert"), None),
        P(("dp", "expert"), None),
        P(("dp", "expert"), None),
        P("expert", None, None),
        P("expert", None, None),
    )
    out_specs = (P(("dp", "expert"), None), P("expert", "dp", None), P("expert", "dp", None))
    return jax.shard_map(
        per_device, mesh=mesh, in_specs=in_specs, out_specs=out_specs, check_vma=False
    )
```

```python
import jax
import jax.numpy as jnp
from jax import lax
from jax.sharding import PartitionSpec as P

TOP = 2


def recompute(input_slots, w_in, hidden_width):
    gate = jnp.einsum(
        "ksd,kdf->ksf", input_slots, w_in[:, :, :hidden_width], preferred_element_type=jnp.float32
    ).astype(jnp.bfloat16).astype(jnp.float32)
    upper = jnp.einsum(
        "ksd,kdf->ksf", input_slots, w_in[:, :, hidden_width:], preferred_element_type=jnp.float32
    ).astype(jnp.bfloat16).astype(jnp.float32)
    sigmoid_gate = jax.nn.sigmoid(gate)
    activated = gate * sigmoid_gate
    hidden = (activated * upper).astype(jnp.bfloat16)
    return (gate, upper, sigmoid_gate, activated, hidden)


def per_device(tokens, cotangent, route_logits, expert_ids, slot_pos, w_in, w_down):
    token_count, width = tokens.shape
    local_experts = w_in.shape[0]
    hidden_width = w_down.shape[1]
    n_expert = lax.axis_size("expert")
    n_dp = lax.axis_size("dp")
    experts_all = local_experts * n_expert
    capacity = 2 * TOP * token_count // experts_all
    first = jax.nn.sigmoid(route_logits[:, 0] - route_logits[:, 1])
    combine = (first, 1.0 - first)
    cotangent_wide = cotangent.astype(jnp.float32)
    destination = (expert_ids * capacity + slot_pos).reshape(-1)
    target = expert_ids * (2 * capacity) + slot_pos
    buffer_row = lax.broadcasted_iota(jnp.int32, (experts_all * 2 * capacity, token_count), 0)
    picks = []
    for k in range(TOP):
        picks.append((buffer_row == target[None, :, k]).astype(jnp.bfloat16))
    token_picks = picks[0] + picks[1]
    send = jnp.dot(token_picks, tokens, preferred_element_type=jnp.float32)
    for k in range(TOP):
        scaled = (combine[k][:, None] * cotangent_wide).astype(jnp.bfloat16)
        shifted = (buffer_row == target[None, :, k] + capacity).astype(jnp.bfloat16)
        send = send + jnp.dot(shifted, scaled, preferred_element_type=jnp.float32)
    send = send.astype(jnp.bfloat16).reshape(experts_all, 2, capacity, width)
    got = lax.all_to_all(send, "expert", split_axis=0, concat_axis=0, tiled=True)
    got = got.reshape(n_expert, local_experts, 2, capacity, width)
    got = jnp.transpose(got, (2, 1, 0, 3, 4)).reshape(2, local_experts, n_expert * capacity, width)
    input_slots, cotangent_slots = got[0], got[1]
    gate, upper, sigmoid_gate, activated, hidden = recompute(input_slots, w_in, hidden_width)
    grad_hidden = jnp.einsum(
        "ksd,kfd->ksf", cotangent_slots, w_down, preferred_element_type=jnp.float32
    )
    term_down = jnp.einsum(
        "ksf,ksd->kfd", hidden, cotangent_slots, preferred_element_type=jnp.float32
    )
    grad_gate = grad_hidden * upper * sigmoid_gate * (1.0 + gate * (1.0 - sigmoid_gate))
    grad_up = grad_hidden * activated
    grad_pair = jnp.concatenate([grad_gate, grad_up], axis=2).astype(jnp.bfloat16)
    term_in = jnp.einsum("ksd,ksf->kdf", input_slots, grad_pair, preferred_element_type=jnp.float32)
    returned = jnp.einsum(
        "ksf,kdf->ksd", grad_pair, w_in, preferred_element_type=jnp.float32
    ).astype(jnp.bfloat16)
    arrived = lax.all_to_all(returned, "expert", split_axis=1, concat_axis=0, tiled=True)
    rows = arrived.reshape(-1, width)[destination].reshape(token_count, TOP, width)
    input_grad = jnp.sum(rows.astype(jnp.float32), axis=1).astype(jnp.bfloat16)
    in_rows, in_cols = term_in.shape[1], term_in.shape[2]
    down_rows, down_cols = term_down.shape[1], term_down.shape[2]
    rows_q = down_rows // n_dp
    main = rows_q * down_cols // in_cols
    spare = in_cols - down_cols
    part_in = term_in.astype(jnp.bfloat16).reshape(local_experts, n_dp, in_rows // n_dp, in_cols)
    part_down = term_down.astype(jnp.bfloat16).reshape(local_experts, n_dp, rows_q, down_cols)
    pieces = [part_down[:, :, main:, c : c + spare] for c in range(0, down_cols, spare)]
    packed = jnp.concatenate([part_down[:, :, :main], jnp.concatenate(pieces, axis=2)], axis=3)
    parts = jnp.concatenate([part_in, packed], axis=2).reshape(local_experts, -1, in_cols)
    summed = lax.psum_scatter(parts, "dp", scatter_dimension=1, tiled=True)
    grad_in = summed[:, : in_rows // n_dp].astype(jnp.float32)
    got_down = summed[:, in_rows // n_dp :]
    rest = rows_q - main
    tail = [got_down[:, i * rest : (i + 1) * rest, down_cols:] for i in range(down_cols // spare)]
    grad_down = jnp.concatenate([got_down[:, :, :down_cols], jnp.concatenate(tail, axis=2)], axis=1)
    grad_down = grad_down.astype(jnp.float32)
    return (input_grad, grad_in, grad_down)


def solution(mesh):
    in_specs = (
        P(("dp", "expert"), None),
        P(("dp", "expert"), None),
        P(("dp", "expert"), None),
        P(("dp", "expert"), None),
        P(("dp", "expert"), None),
        P("expert", None, None),
        P("expert", None, None),
    )
    out_specs = (P(("dp", "expert"), None), P("expert", "dp", None), P("expert", "dp", None))
    return jax.shard_map(
        per_device, mesh=mesh, in_specs=in_specs, out_specs=out_specs, check_vma=False
    )
```

```python
import functools

import jax
import jax.numpy as jnp
from jax import lax
from jax.experimental import pallas as pl
from jax.experimental.pallas import tpu as pltpu
from jax.sharding import PartitionSpec as P

TOP = 2


def recompute(input_slots, w_in, hidden_width):
    gate = jnp.einsum(
        "ksd,kdf->ksf", input_slots, w_in[:, :, :hidden_width], preferred_element_type=jnp.float32
    )
    upper = jnp.einsum(
        "ksd,kdf->ksf", input_slots, w_in[:, :, hidden_width:], preferred_element_type=jnp.float32
    )
    sigmoid_gate = jax.nn.sigmoid(gate)
    activated = gate * sigmoid_gate
    hidden = (activated * upper).astype(jnp.bfloat16)
    return (gate, upper, sigmoid_gate, activated, hidden)


def pack_kernel(main, spare, in_ref, down_ref, out_ref, sems):
    experts, _, in_rows, in_cols = in_ref.shape
    down_rows, down_cols = down_ref.shape[2], down_ref.shape[3]
    rest = down_rows - main
    copies = []
    for k in range(experts):
        pairs = [
            (in_ref.at[k], out_ref.at[k, :, pl.ds(0, in_rows), :]),
            (down_ref.at[k, :, pl.ds(0, main), :], out_ref.at[k, :, pl.ds(in_rows, main), pl.ds(0, down_cols)]),
        ]
        for i, c in enumerate(range(0, down_cols, spare)):
            pairs.append((
                down_ref.at[k, :, pl.ds(main, rest), pl.ds(c, spare)],
                out_ref.at[k, :, pl.ds(in_rows + i * rest, rest), pl.ds(down_cols, spare)],
            ))
        for src, dst in pairs:
            copy = pltpu.make_async_copy(src, dst, sems.at[len(copies)])
            copy.start()
            copies.append(copy)
    for copy in copies:
        copy.wait()


def pack(part_in, part_down, main, spare):
    experts, n_dp, in_rows, in_cols = part_in.shape
    n_copies = experts * (2 + part_down.shape[3] // spare)
    nbytes = 2 * (part_in.size + part_down.size) * part_in.dtype.itemsize
    return pl.pallas_call(
        functools.partial(pack_kernel, main, spare),
        out_shape=jax.ShapeDtypeStruct((experts, n_dp, in_rows + main, in_cols), part_in.dtype),
        in_specs=[pl.BlockSpec(memory_space=pl.ANY)] * 2,
        out_specs=pl.BlockSpec(memory_space=pl.ANY),
        scratch_shapes=[pltpu.SemaphoreType.DMA((n_copies,))],
        cost_estimate=pl.CostEstimate(flops=0, bytes_accessed=nbytes, transcendentals=0),
    )(part_in, part_down)


def per_device(tokens, cotangent, route_logits, expert_ids, slot_pos, w_in, w_down):
    token_count, width = tokens.shape
    local_experts = w_in.shape[0]
    hidden_width = w_down.shape[1]
    n_expert = lax.axis_size("expert")
    n_dp = lax.axis_size("dp")
    experts_all = local_experts * n_expert
    capacity = 2 * TOP * token_count // experts_all
    first = jax.nn.sigmoid(route_logits[:, 0] - route_logits[:, 1])
    combine = (first, 1.0 - first)
    cotangent_wide = cotangent.astype(jnp.float32)
    destination = (expert_ids * capacity + slot_pos).reshape(-1)
    target = expert_ids * (2 * capacity) + slot_pos
    buffer_row = lax.broadcasted_iota(jnp.int32, (experts_all * 2 * capacity, token_count), 0)
    picks = []
    for k in range(TOP):
        picks.append((buffer_row == target[None, :, k]).astype(jnp.bfloat16))
    token_picks = picks[0] + picks[1]
    send = jnp.dot(token_picks, tokens, preferred_element_type=jnp.float32)
    for k in range(TOP):
        scaled = (combine[k][:, None] * cotangent_wide).astype(jnp.bfloat16)
        shifted = (buffer_row == target[None, :, k] + capacity).astype(jnp.bfloat16)
        send = send + jnp.dot(shifted, scaled, preferred_element_type=jnp.float32)
    send = send.astype(jnp.bfloat16).reshape(experts_all, 2, capacity, width)
    got = lax.all_to_all(send, "expert", split_axis=0, concat_axis=0, tiled=True)
    got = got.reshape(n_expert, local_experts, 2, capacity, width)
    got = jnp.transpose(got, (2, 1, 0, 3, 4)).reshape(2, local_experts, n_expert * capacity, width)
    input_slots, cotangent_slots = got[0], got[1]
    gate, upper, sigmoid_gate, activated, hidden = recompute(input_slots, w_in, hidden_width)
    grad_hidden = jnp.einsum(
        "ksd,kfd->ksf", cotangent_slots, w_down, preferred_element_type=jnp.float32
    )
    term_down = jnp.einsum(
        "ksf,ksd->kfd", hidden, cotangent_slots, preferred_element_type=jnp.float32
    )
    grad_gate = grad_hidden * upper * sigmoid_gate * (1.0 + gate * (1.0 - sigmoid_gate))
    grad_up = grad_hidden * activated
    grad_pair = jnp.concatenate([grad_gate, grad_up], axis=2).astype(jnp.bfloat16)
    term_in = jnp.einsum("ksd,ksf->kdf", input_slots, grad_pair, preferred_element_type=jnp.float32)
    returned = jnp.einsum(
        "ksf,kdf->ksd", grad_pair, w_in, preferred_element_type=jnp.float32
    ).astype(jnp.bfloat16)
    arrived = lax.all_to_all(returned, "expert", split_axis=1, concat_axis=0, tiled=True)
    rows = arrived.reshape(-1, width)[destination].reshape(token_count, TOP, width)
    input_grad = jnp.sum(rows.astype(jnp.float32), axis=1).astype(jnp.bfloat16)
    in_rows, in_cols = term_in.shape[1], term_in.shape[2]
    down_rows, down_cols = term_down.shape[1], term_down.shape[2]
    rows_q = down_rows // n_dp
    main = rows_q * down_cols // in_cols
    spare = in_cols - down_cols
    part_in = term_in.astype(jnp.bfloat16).reshape(local_experts, n_dp, in_rows // n_dp, in_cols)
    part_down = term_down.astype(jnp.bfloat16).reshape(local_experts, n_dp, rows_q, down_cols)
    parts = pack(part_in, part_down, main, spare).reshape(local_experts, -1, in_cols)
    summed = lax.psum_scatter(parts, "dp", scatter_dimension=1, tiled=True)
    grad_in = summed[:, : in_rows // n_dp].astype(jnp.float32)
    got_down = summed[:, in_rows // n_dp :]
    rest = rows_q - main
    tail = [got_down[:, i * rest : (i + 1) * rest, down_cols:] for i in range(down_cols // spare)]
    grad_down = jnp.concatenate([got_down[:, :, :down_cols], jnp.concatenate(tail, axis=2)], axis=1)
    grad_down = grad_down.astype(jnp.float32)
    return (input_grad, grad_in, grad_down)


def solution(mesh):
    in_specs = (
        P(("dp", "expert"), None),
        P(("dp", "expert"), None),
        P(("dp", "expert"), None),
        P(("dp", "expert"), None),
        P(("dp", "expert"), None),
        P("expert", None, None),
        P("expert", None, None),
    )
    out_specs = (P(("dp", "expert"), None), P("expert", "dp", None), P("expert", "dp", None))
    return jax.shard_map(
        per_device, mesh=mesh, in_specs=in_specs, out_specs=out_specs, check_vma=False
    )
```

```python
import jax
import jax.numpy as jnp
from jax import lax
from jax.sharding import PartitionSpec as P

TOP = 2


def recompute(input_slots, w_in, hidden_width):
    gate = jnp.einsum(
        "ksd,kdf->ksf", input_slots, w_in[:, :, :hidden_width], preferred_element_type=jnp.float32
    )
    upper = jnp.einsum(
        "ksd,kdf->ksf", input_slots, w_in[:, :, hidden_width:], preferred_element_type=jnp.float32
    )
    sigmoid_gate = jax.nn.sigmoid(gate)
    activated = gate * sigmoid_gate
    hidden = (activated * upper).astype(jnp.bfloat16)
    return (gate, upper, sigmoid_gate, activated, hidden)


def per_device(tokens, cotangent, route_logits, expert_ids, slot_pos, w_in, w_down):
    token_count, width = tokens.shape
    local_experts = w_in.shape[0]
    hidden_width = w_down.shape[1]
    n_expert = lax.axis_size("expert")
    n_dp = lax.axis_size("dp")
    experts_all = local_experts * n_expert
    capacity = 2 * TOP * token_count // experts_all
    first = jax.nn.sigmoid(route_logits[:, 0] - route_logits[:, 1])
    combine = (first, 1.0 - first)
    cotangent_wide = cotangent.astype(jnp.float32)
    destination = (expert_ids * capacity + slot_pos).reshape(-1)
    target = expert_ids * (2 * capacity) + slot_pos
    buffer_row = lax.broadcasted_iota(jnp.int32, (experts_all * 2 * capacity, token_count), 0)
    picks = []
    for k in range(TOP):
        picks.append((buffer_row == target[None, :, k]).astype(jnp.bfloat16))
    token_picks = picks[0] + picks[1]
    send = jnp.dot(token_picks, tokens, preferred_element_type=jnp.bfloat16)
    for k in range(TOP):
        scaled = (combine[k][:, None] * cotangent_wide).astype(jnp.bfloat16)
        shifted = (buffer_row == target[None, :, k] + capacity).astype(jnp.bfloat16)
        send = send + jnp.dot(shifted, scaled, preferred_element_type=jnp.bfloat16)
    send = send.reshape(experts_all, 2, capacity, width)
    got = lax.all_to_all(send, "expert", split_axis=0, concat_axis=0, tiled=True)
    got = got.reshape(n_expert, local_experts, 2, capacity, width)
    got = jnp.transpose(got, (2, 1, 0, 3, 4)).reshape(2, local_experts, n_expert * capacity, width)
    input_slots, cotangent_slots = got[0], got[1]
    gate, upper, sigmoid_gate, activated, hidden = recompute(input_slots, w_in, hidden_width)
    grad_hidden = jnp.einsum(
        "ksd,kfd->ksf", cotangent_slots, w_down, preferred_element_type=jnp.float32
    )
    term_down = jnp.einsum(
        "ksf,ksd->kfd", hidden, cotangent_slots, preferred_element_type=jnp.float32
    )
    grad_gate = grad_hidden * upper * sigmoid_gate * (1.0 + gate * (1.0 - sigmoid_gate))
    grad_up = grad_hidden * activated
    grad_pair = jnp.concatenate([grad_gate, grad_up], axis=2).astype(jnp.bfloat16)
    term_in = jnp.einsum("ksd,ksf->kdf", input_slots, grad_pair, preferred_element_type=jnp.float32)
    returned = jnp.einsum(
        "ksf,kdf->ksd", grad_pair, w_in, preferred_element_type=jnp.float32
    ).astype(jnp.bfloat16)
    arrived = lax.all_to_all(returned, "expert", split_axis=1, concat_axis=0, tiled=True)
    rows = arrived.reshape(-1, width)[destination].reshape(token_count, TOP, width)
    input_grad = jnp.sum(rows.astype(jnp.float32), axis=1).astype(jnp.bfloat16)
    in_rows, in_cols = term_in.shape[1], term_in.shape[2]
    down_rows, down_cols = term_down.shape[1], term_down.shape[2]
    rows_q = down_rows // n_dp
    main = rows_q * down_cols // in_cols
    spare = in_cols - down_cols
    part_in = term_in.astype(jnp.bfloat16).reshape(local_experts, n_dp, in_rows // n_dp, in_cols)
    part_down = term_down.astype(jnp.bfloat16).reshape(local_experts, n_dp, rows_q, down_cols)
    pieces = [part_down[:, :, main:, c : c + spare] for c in range(0, down_cols, spare)]
    packed = jnp.concatenate([part_down[:, :, :main], jnp.concatenate(pieces, axis=2)], axis=3)
    parts = jnp.concatenate([part_in, packed], axis=2).reshape(local_experts, -1, in_cols)
    summed = lax.psum_scatter(parts, "dp", scatter_dimension=1, tiled=True)
    grad_in = summed[:, : in_rows // n_dp].astype(jnp.float32)
    got_down = summed[:, in_rows // n_dp :]
    rest = rows_q - main
    tail = [got_down[:, i * rest : (i + 1) * rest, down_cols:] for i in range(down_cols // spare)]
    grad_down = jnp.concatenate([got_down[:, :, :down_cols], jnp.concatenate(tail, axis=2)], axis=1)
    grad_down = grad_down.astype(jnp.float32)
    return (input_grad, grad_in, grad_down)


def solution(mesh):
    in_specs = (
        P(("dp", "expert"), None),
        P(("dp", "expert"), None),
        P(("dp", "expert"), None),
        P(("dp", "expert"), None),
        P(("dp", "expert"), None),
        P("expert", None, None),
        P("expert", None, None),
    )
    out_specs = (P(("dp", "expert"), None), P("expert", "dp", None), P("expert", "dp", None))
    return jax.shard_map(
        per_device, mesh=mesh, in_specs=in_specs, out_specs=out_specs, check_vma=False
    )
```
